32 devices in a mesh: dp: 2 (over x), ctx: 16 (over z, y, core).
Axes of the slice: x: 2, y: 2, z: 4, core: 2. Of those that a mesh axis runs over, the one named last changes fastest.
Arguments:
- queries: bfloat16 [2, 6144, 4096], P('dp', 'ctx'), may hold values from -6 to 6
- keys: bfloat16 [2, 6144, 4096], P('dp', 'ctx'), may hold values from -6 to 6
- values: bfloat16 [2, 6144, 4096], P('dp', 'ctx'), may hold values from -6 to 6
- out_grad: bfloat16 [2, 6144, 4096], P('dp', 'ctx'), may hold values from -15 to 15
- gain: float32 [4096], replicated, may hold values from 0.1 to 1.9
Outputs:
- output: bfloat16 [2, 6144, 4096], P('dp', 'ctx')
- grad_queries: bfloat16 [2, 6144, 4096], P('dp', 'ctx')
- grad_keys: bfloat16 [2, 6144, 4096], P('dp', 'ctx')
- grad_values: bfloat16 [2, 6144, 4096], P('dp', 'ctx')
- grad_gain: float32 [4096], replicated
The draws below stay inside these ranges and needn't reach their ends.
All inputs are finite; a program needn't handle non-finite values.
Results may differ from the reference program's by a relative error of at most 0.007.
Values sent between devices are 32-bit elements; how exact they have to be, the bound alone decides.
A program may use at most 256 MiB of HBM per device.

```python
import jax
import jax.numpy as jnp
from jax import lax

HEADS = 32
HD = 128
TOK_DEV = 384
TOKENS = 6144
SEQS = 2
N_CTX = 16


def draw_out_grad(key, part):
    position = jnp.arange(TOKENS, dtype=jnp.float32) / TOKENS
    scaling = (1.0 + 2.0 * position)[None, :, None]
    result = jnp.clip(jax.random.normal(key, (SEQS, TOKENS, HEADS * HD), jnp.float32), -5.0, 5.0) * scaling
    return result.astype(jnp.bfloat16)


def level_of(own_key, extent, cuts, least, top_value):
    def one(dim, shards_of):
        heights = jax.random.uniform(jax.random.fold_in(jax.random.fold_in(own_key, 6), dim), (shards_of,), jnp.float32, least / len(cuts), top_value / len(cuts))
        return jnp.repeat(jnp.exp(heights), extent[dim] // shards_of).reshape((-1,) + (1,) * (len(extent) - dim - 1))

    loudness = one(*cuts[0])
    for cut in cuts[1:]:
        loudness = loudness * one(*cut)
    return loudness


def scatter_about(rng, dims, scale, most, pieces=(), kind=jnp.bfloat16):
    array = scale * jax.random.normal(rng, dims, jnp.float32)
    if pieces:
        array = array * level_of(rng, dims, pieces, -0.22, 0.18)
    return jnp.clip(array, -most, most).astype(kind)


def setup_inputs(seed: int = 0) -> dict:
    seeds = jax.random.split(jax.random.key(seed), 6)
    return {
        "queries": scatter_about(seeds[0], (SEQS, TOKENS, HEADS * HD), 1.0, 6.0, ((0, 2), (1, 16))),
        "keys": scatter_about(seeds[1], (SEQS, TOKENS, HEADS * HD), 1.0, 6.0, ((0, 2), (1, 16))),
        "values": scatter_about(seeds[2], (SEQS, TOKENS, HEADS * HD), 1.0, 6.0, ((0, 2), (1, 16))),
        "out_grad": draw_out_grad(jax.random.fold_in(seeds[5], 71), 0),
        "gain": jnp.clip(1.0 + 0.18 * jax.random.normal(seeds[4], (HEADS * HD,), jnp.float32), 0.1, 1.9),
    }


EPS = 1e-06
HIGH = lax.Precision.HIGHEST

def causal_mask(length):
    row_index = lax.broadcasted_iota(jnp.int32, (length, length), 0)
    col_index = lax.broadcasted_iota(jnp.int32, (length, length), 1)
    return row_index >= col_index

def score_block(query, key_rows):
    scores = jnp.einsum('ihd,jhd->hij', query.astype(jnp.float32), key_rows.astype(jnp.float32), precision=HIGH)
    return jnp.where(causal_mask(query.shape[0])[None], scores, 0.0).astype(jnp.bfloat16)

def forward_block(items):
    query, key_rows, value, grad_out, prefix_bf, gain_rows = items
    scores = score_block(query, key_rows)
    attended = jnp.einsum('hij,jhe->ihe', scores.astype(jnp.float32), value.astype(jnp.float32), precision=HIGH)
    attended = attended + jnp.einsum('ihd,hde->ihe', query.astype(jnp.float32), prefix_bf.astype(jnp.float32), precision=HIGH)
    inverse = lax.rsqrt(lax.optimization_barrier(jnp.mean(attended * attended, axis=-1, keepdims=True)) + EPS)
    normed = attended * inverse
    output = (normed * gain_rows).astype(jnp.bfloat16)
    grad_float = grad_out.astype(jnp.float32)
    gain_term = lax.optimization_barrier(jnp.sum(grad_float * normed, axis=0))
    scaled = grad_float * gain_rows
    dattn = (inverse * (scaled - normed * lax.optimization_barrier(jnp.mean(scaled * normed, axis=-1, keepdims=True)))).astype(jnp.bfloat16)
    gstate = jnp.einsum('ihd,ihe->hde', query.astype(jnp.float32), dattn.astype(jnp.float32), precision=HIGH)
    return (output, dattn, gain_term, gstate)

def backward_block(items):
    query, key_rows, value, dattn, prefix_bf, suffix_bf = items
    query_f = query.astype(jnp.float32)
    key_f = key_rows.astype(jnp.float32)
    value_f = value.astype(jnp.float32)
    dattn_f = dattn.astype(jnp.float32)
    scores = score_block(query, key_rows).astype(jnp.float32)
    dscore = jnp.einsum('ihe,jhe->hij', dattn_f, value_f, precision=HIGH)
    dscore = jnp.where(causal_mask(query.shape[0])[None], dscore, 0.0).astype(jnp.bfloat16).astype(jnp.float32)
    prefix_f = prefix_bf.astype(jnp.float32)
    suffix_f = suffix_bf.astype(jnp.float32)
    grad_q = jnp.einsum('hij,jhd->ihd', dscore, key_f, precision=HIGH) + jnp.einsum('ihe,hde->ihd', dattn_f, prefix_f, precision=HIGH)
    grad_k = jnp.einsum('hij,ihd->jhd', dscore, query_f, precision=HIGH) + jnp.einsum('jhe,hde->jhd', value_f, suffix_f, precision=HIGH)
    grad_v = jnp.einsum('hij,ihe->jhe', scores, dattn_f, precision=HIGH) + jnp.einsum('jhd,hde->jhe', key_f, suffix_f, precision=HIGH)
    return (grad_q.astype(jnp.bfloat16), grad_k.astype(jnp.bfloat16), grad_v.astype(jnp.bfloat16))

def reference(queries, keys, values, out_grad, gain):
    gain_rows = gain.reshape(HEADS, HD)
    shape4 = (N_CTX, TOK_DEV, HEADS, HD)
    outputs, grads_q, grads_k, grads_v = ([], [], [], [])
    grad_gain = jnp.zeros((HEADS, HD), jnp.float32)
    for seq in range(SEQS):
        query = queries[seq].reshape(shape4)
        key_rows = keys[seq].reshape(shape4)
        value = values[seq].reshape(shape4)
        grad_out = out_grad[seq].reshape(shape4)
        states = jnp.einsum('bjhd,bjhe->bhde', key_rows.astype(jnp.float32), value.astype(jnp.float32), precision=HIGH)
        zeros = jnp.zeros((1, HEADS, HD, HD), jnp.float32)
        prefix = jnp.concatenate([zeros, jnp.cumsum(states, axis=0)[:-1]], axis=0).astype(jnp.bfloat16)
        gain_many = jnp.broadcast_to(gain_rows, (N_CTX, HEADS, HD))
        output, dattn, gain_terms, gstates = lax.map(forward_block, (query, key_rows, value, grad_out, prefix, gain_many))
        grad_gain = grad_gain + lax.optimization_barrier(jnp.sum(gain_terms, axis=0))
        inclusive = jnp.cumsum(gstates[::-1], axis=0)[::-1]
        suffix = jnp.concatenate([inclusive[1:], zeros], axis=0).astype(jnp.bfloat16)
        grad_q, grad_k, grad_v = lax.map(backward_block, (query, key_rows, value, dattn, prefix, suffix))
        outputs.append(output.reshape(TOKENS, HEADS * HD))
        grads_q.append(grad_q.reshape(TOKENS, HEADS * HD))
        grads_k.append(grad_k.reshape(TOKENS, HEADS * HD))
        grads_v.append(grad_v.reshape(TOKENS, HEADS * HD))
    return (jnp.stack(outputs), jnp.stack(grads_q), jnp.stack(grads_k), jnp.stack(grads_v), grad_gain.reshape(HEADS * HD))
```

```python
import functools

import jax
import jax.numpy as jnp
from jax import lax
from jax.experimental import pallas as pl
from jax.experimental.pallas import tpu as pltpu
from jax.sharding import PartitionSpec as P

HD = 128
PW = 2 * HD
EPS = 1e-06
F32 = jnp.float32
BF16 = jnp.bfloat16
MESH = pl.DeviceIdType.MESH

LAG_FWD = 2
LAG_GY = 4
LAG_GZ = 6
LAG_STEP = 4
LAG_FIN = 2
LAG_PRO = 3


def nt(a, b):
    return lax.dot_general(a, b, (((1,), (1,)), ((), ())), preferred_element_type=F32)


def nn(a, b):
    return lax.dot_general(a, b, (((1,), (0,)), ((), ())), preferred_element_type=F32)


def tn(a, b):
    return lax.dot_general(a, b, (((0,), (0,)), ((), ())), preferred_element_type=F32)


def kernel(
    ndp, nctx, pairs,
    q_hbm, k_hbm, v_hbm, g_hbm, gain_ref,
    o_hbm, gq_hbm, gk_hbm, gv_hbm, gg_ref,
    qb, kb, vb, gb, gki, gvi,
    s_all, x_in, c_out, y_in, e_in, e_out, p_out, p_all,
    t_all, tx_in, tc_out, ty_in, te_in, te_out, tp_out, tp_all,
    gsum, grecv,
    io_sem, send_sem, recv_sem, gs_sem, gr_sem,
):
    dp = lax.axis_index("dp")
    me = lax.axis_index("ctx")
    c = lax.rem(me, 2)
    y = lax.rem(me // 2, 2)
    z = me // 4
    nz = nctx // 4
    sib = (dp, me + 1 - 2 * c)
    ypeer = (dp, me + 2 - 4 * y)
    up = (dp, lax.min(me + 4, nctx - 1))
    down = (dp, lax.max(me - 4, 0))
    length = qb.shape[1]

    steps = []
    bit = 1
    while bit < ndp:
        steps.append((dp + bit - 2 * bit * lax.rem(dp // bit, 2), me))
        bit *= 2
    n_dp = len(steps)
    bit = 1
    while bit < nctx:
        steps.append((dp, me + bit - 2 * bit * lax.rem(me // bit, 2)))
        bit *= 2

    def loads(p):
        cols = pl.ds(pl.multiple_of(p * PW, PW), PW)
        return [
            pltpu.make_async_copy(h.at[0, :, cols], b.at[p], io_sem.at[i, p])
            for i, (h, b) in enumerate(((k_hbm, kb), (v_hbm, vb), (q_hbm, qb), (g_hbm, gb)))
        ]

    def stores(p):
        cols = pl.ds(pl.multiple_of(p * PW, PW), PW)
        return [
            pltpu.make_async_copy(b.at[p], h.at[0, :, cols], io_sem.at[i, p])
            for i, (h, b) in enumerate(((gk_hbm, kb), (gv_hbm, vb), (gq_hbm, qb), (o_hbm, gb)))
        ]

    def hop(kind, src, dst, p, to):
        return pltpu.make_async_remote_copy(
            src_ref=src, dst_ref=dst, send_sem=send_sem.at[kind], recv_sem=recv_sem.at[kind, p],
            device_id=to, device_id_type=MESH,
        )

    def load_kv(p, _):
        for copy in loads(p)[:2]:
            copy.start()
        return 0

    def load_qg(p, _):
        for copy in loads(p)[2:]:
            copy.start()
        return 0

    lax.fori_loop(0, pairs, load_kv, 0)
    lax.fori_loop(0, pairs, load_qg, 0)

    barrier = pltpu.get_barrier_semaphore()
    greet = [sib, ypeer] + steps[:n_dp] + steps[n_dp + 3:]
    for other in greet:
        pl.semaphore_signal(barrier, inc=1, device_id=other, device_id_type=MESH)

    @pl.when(z < nz - 1)
    def _():
        pl.semaphore_signal(barrier, inc=1, device_id=up, device_id_type=MESH)

    @pl.when(z > 0)
    def _():
        pl.semaphore_signal(barrier, inc=1, device_id=down, device_id_type=MESH)

    expected = len(greet) + lax.min(z, 1) + lax.min(nz - 1 - z, 1)
    pl.semaphore_wait(barrier, expected)

    @pl.when(z == 0)
    def _():
        e_in[...] = jnp.zeros_like(e_in)

    @pl.when(z == nz - 1)
    def _():
        te_in[...] = jnp.zeros_like(te_in)

    def to_chip(p, kind, all_ref, in_ref):
        return hop(kind, all_ref.at[1 - c, p], in_ref.at[p], p, sib)

    def chip_total(p, kind, all_ref, in_ref, out_ref, y_ref):
        to_chip(p, kind, all_ref, in_ref).wait_recv()
        out_ref[p] = all_ref[c, p] + in_ref[p]
        hop(kind + 1, out_ref.at[p], y_ref.at[p], p, ypeer).start()

    def along(p, kind, all_ref, in_ref, out_ref, y_ref, e_ref, eo_ref, po_ref, pa_ref, reverse):
        first = nz - 1 if reverse else 0
        last = nz - 1 - first
        to = down if reverse else up
        hop(kind + 1, out_ref.at[p], y_ref.at[p], p, ypeer).wait_recv()

        @pl.when(z != first)
        def _():
            hop(kind + 2, eo_ref.at[p], e_ref.at[p], p, to).wait_recv()

        entering = e_ref[p]
        across = y_ref[p]

        @pl.when(z != last)
        def _():
            eo_ref[p] = entering + (out_ref[p] + across)
            hop(kind + 2, eo_ref.at[p], e_ref.at[p], p, to).start()

        has_y = (y == 0) if reverse else (y == 1)
        mine_later = (c == 0) if reverse else (c == 1)
        base = entering + jnp.where(has_y, across, 0.0)
        po_ref[p] = base + jnp.where(mine_later, 0.0, all_ref[c, p])
        hop(kind + 3, po_ref.at[p], pa_ref.at[c, p], p, sib).start()
        pa_ref[c, p] = base + jnp.where(mine_later, in_ref[p], 0.0)

    fwd = (0, s_all, x_in, c_out, y_in)
    bwd = (4, t_all, tx_in, tc_out, ty_in)

    def prologue(t, _):
        @pl.when(t < pairs)
        def _():
            for copy in loads(t)[:2]:
                copy.wait()
            for j in range(2):
                at = slice(j * HD, (j + 1) * HD)
                s_all[j, t] = tn(kb[t, :, at], vb[t, :, at])
            to_chip(t, 0, s_all, x_in).start()

        @pl.when(t >= LAG_PRO)
        def _():
            chip_total(t - LAG_PRO, *fwd)
        return 0

    lax.fori_loop(0, pairs + LAG_PRO, prologue, 0)

    def forward(p):
        for copy in loads(p)[2:]:
            copy.wait()
        hop(3, p_out.at[p], p_all.at[1 - c, p], p, sib).wait_recv()
        row = lax.broadcasted_iota(jnp.int32, (length, length), 0)
        col = lax.broadcasted_iota(jnp.int32, (length, length), 1)
        causal = row >= col
        kept = []
        for j in range(2):
            at = slice(j * HD, (j + 1) * HD)
            lanes = pl.ds(pl.multiple_of(p * PW + j * HD, HD), HD)
            query, key_rows, value = qb[p, :, at], kb[p, :, at], vb[p, :, at]
            prefix = p_all[j, p].astype(BF16)
            scores = jnp.where(causal, nt(query, key_rows), 0.0).astype(BF16)
            attended = nn(scores, value) + nn(query, prefix)
            inverse = lax.rsqrt(jnp.mean(attended * attended, axis=-1, keepdims=True) + EPS)
            normed = attended * inverse
            gain = gain_ref[:, lanes]
            grad = gb[p, :, at].astype(F32)
            gsum[0, :, lanes] = jnp.sum(grad * normed, axis=0, keepdims=True)
            scaled = grad * gain
            dattn = (
                inverse * (scaled - normed * jnp.mean(scaled * normed, axis=-1, keepdims=True))
            ).astype(BF16)
            gb[p, :, at] = (normed * gain).astype(BF16)
            t_all[j, p] = tn(query, dattn)
            kept.append((query, key_rows, value, prefix, scores, dattn))
        to_chip(p, 4, t_all, tx_in).start()
        for j in range(2):
            at = slice(j * HD, (j + 1) * HD)
            query, key_rows, value, prefix, scores, dattn = kept[j]
            dscore = jnp.where(causal, nt(dattn, value), 0.0).astype(BF16)
            grad_q = nn(dscore, key_rows) + nt(dattn, prefix)
            gki[p, :, at] = tn(dscore, query)
            gvi[p, :, at] = tn(scores, dattn)
            qb[p, :, at] = grad_q.astype(BF16)
        for copy in stores(p)[2:]:
            copy.start()

    def final(p):
        hop(7, tp_out.at[p], tp_all.at[1 - c, p], p, sib).wait_recv()
        for j in range(2):
            at = slice(j * HD, (j + 1) * HD)
            key_rows, value = kb[p, :, at], vb[p, :, at]
            suffix = tp_all[j, p].astype(BF16)
            kb[p, :, at] = (gki[p, :, at] + nt(value, suffix)).astype(BF16)
            vb[p, :, at] = (gvi[p, :, at] + nn(key_rows, suffix)).astype(BF16)
        for copy in stores(p)[:2]:
            copy.start()

    def gain_hop(i):
        return pltpu.make_async_remote_copy(
            src_ref=gsum.at[i], dst_ref=grecv.at[i], send_sem=gs_sem.at[i], recv_sem=gr_sem.at[i],
            device_id=steps[i], device_id_type=MESH,
        )

    lag_gz = LAG_GZ + LAG_STEP * (nz - 1 - z)
    gain_at = pairs + LAG_FWD
    total = max(
        pairs + LAG_GZ + LAG_STEP * (nz - 1) + LAG_FIN,
        gain_at + 2 * len(steps) + 1,
    )

    def guarded(p, stage):
        @pl.when(jnp.logical_and(p >= 0, p < pairs))
        def _():
            stage(p)

    def main(t, _):
        guarded(t, lambda p: along(p, *fwd, e_in, e_out, p_out, p_all, False))
        guarded(t - LAG_FWD, forward)
        guarded(t - LAG_GY, lambda p: chip_total(p, *bwd))
        guarded(t - lag_gz, lambda p: along(p, *bwd, te_in, te_out, tp_out, tp_all, True))
        guarded(t - lag_gz - LAG_FIN, final)
        for i in range(len(steps) + 1):
            @pl.when(t == gain_at + 2 * i)
            def _():
                if i > 0:
                    gain_hop(i - 1).wait_recv()
                    gsum[i] = gsum[i - 1] + grecv[i - 1]
                if i < len(steps):
                    gain_hop(i).start()
        return 0

    lax.fori_loop(0, total, main, 0)
    gg_ref[...] = gsum[len(steps)]

    for i in range(len(steps)):
        gain_hop(i).wait_send()
    for kind, all_ref, in_ref, out_ref, y_ref, eo_ref, e_ref, po_ref, pa_ref in (
        (*fwd, e_out, e_in, p_out, p_all),
        (*bwd, te_out, te_in, tp_out, tp_all),
    ):
        hop(kind, all_ref.at[1 - c], in_ref, 0, sib).wait_send()
        hop(kind + 1, out_ref, y_ref, 0, ypeer).wait_send()
        reverse = kind == 4

        @pl.when(z != (0 if reverse else nz - 1))
        def _():
            hop(kind + 2, eo_ref, e_ref, 0, down if reverse else up).wait_send()

        hop(kind + 3, po_ref, pa_ref.at[c], 0, sib).wait_send()

    def finish(p, _):
        for copy in stores(p):
            copy.wait()
        return 0

    lax.fori_loop(0, pairs, finish, 0)


def body(ndp, nctx, queries, keys, values, out_grad, gain):
    _, length, width = queries.shape
    pairs = width // PW
    nsteps = (ndp - 1).bit_length() + (nctx - 1).bit_length()
    tile = pltpu.VMEM((pairs, length, PW), BF16)
    wide = pltpu.VMEM((pairs, length, PW), F32)
    one = pltpu.VMEM((pairs, HD, HD), F32)
    two = pltpu.VMEM((2, pairs, HD, HD), F32)
    states = [two, one, one, one, one, one, one, two]
    hbm = pl.BlockSpec(memory_space=pl.ANY)
    vmem = pl.BlockSpec(memory_space=pltpu.VMEM)
    big = jax.ShapeDtypeStruct(queries.shape, BF16)
    out = pl.pallas_call(
        functools.partial(kernel, ndp, nctx, pairs),
        out_shape=(big, big, big, big, jax.ShapeDtypeStruct((1, width), F32)),
        in_specs=[hbm, hbm, hbm, hbm, vmem],
        out_specs=(hbm, hbm, hbm, hbm, vmem),
        scratch_shapes=[
            tile, tile, tile, tile, wide, wide, *states, *states,
            pltpu.VMEM((nsteps + 1, 1, width), F32),
            pltpu.VMEM((nsteps, 1, width), F32),
            pltpu.SemaphoreType.DMA((4, pairs)),
            pltpu.SemaphoreType.DMA((8,)),
            pltpu.SemaphoreType.DMA((8, pairs)),
            pltpu.SemaphoreType.DMA((nsteps,)),
            pltpu.SemaphoreType.DMA((nsteps,)),
        ],
        compiler_params=pltpu.CompilerParams(
            collective_id=0, has_side_effects=True, vmem_limit_bytes=56 << 20
        ),
        name="lightning",
    )(queries, keys, values, out_grad, gain.reshape(1, width))
    return (*out[:4], out[4].reshape(width))


def solution(mesh):
    split = P("dp", "ctx", None)
    return jax.shard_map(
        functools.partial(body, mesh.shape["dp"], mesh.shape["ctx"]),
        mesh=mesh,
        in_specs=(split, split, split, split, P()),
        out_specs=(split, split, split, split, P()),
        check_vma=False,
    )
```

```python
import functools

import jax
import jax.numpy as jnp
from jax import lax
from jax.experimental import pallas as pl
from jax.experimental.pallas import tpu as pltpu
from jax.sharding import PartitionSpec as P

HD = 128
PW = 2 * HD
EPS = 1e-06
F32 = jnp.float32
BF16 = jnp.bfloat16
MESH = pl.DeviceIdType.MESH

LAG_FWD = 2
LAG_GY = 4
LAG_GZ = 6
LAG_STEP = 4
LAG_FIN = 2
LAG_PRO = 3
LAG_TURN = 4


def nt(a, b):
    return lax.dot_general(a, b, (((1,), (1,)), ((), ())), preferred_element_type=F32)


def nn(a, b):
    return lax.dot_general(a, b, (((1,), (0,)), ((), ())), preferred_element_type=F32)


def tn(a, b):
    return lax.dot_general(a, b, (((0,), (0,)), ((), ())), preferred_element_type=F32)


def kernel(
    ndp, nctx, pairs,
    q_hbm, k_hbm, v_hbm, g_hbm, gain_ref,
    o_hbm, gq_hbm, gk_hbm, gv_hbm, gg_ref,
    qb, kb, vb, gb, kept, held,
    s_all, x_in, c_out, y_in, e_in, e_out, p_out, p_all,
    t_all, tx_in, tc_out, ty_in, te_in, te_out, tp_out, tp_all,
    gsum, grecv,
    io_sem, send_sem, recv_sem, gs_sem, gr_sem,
):
    dp = lax.axis_index("dp")
    me = lax.axis_index("ctx")
    c = lax.rem(me, 2)
    y = lax.rem(me // 2, 2)
    z = me // 4
    nz = nctx // 4
    sib = (dp, me + 1 - 2 * c)
    ypeer = (dp, me + 2 - 4 * y)
    up = (dp, lax.min(me + 4, nctx - 1))
    down = (dp, lax.max(me - 4, 0))
    length = qb.shape[1]

    steps = []
    bit = 1
    while bit < ndp:
        steps.append((dp + bit - 2 * bit * lax.rem(dp // bit, 2), me))
        bit *= 2
    n_dp = len(steps)
    bit = 1
    while bit < nctx:
        steps.append((dp, me + bit - 2 * bit * lax.rem(me // bit, 2)))
        bit *= 2

    def loads(p):
        cols = pl.ds(pl.multiple_of(p * PW, PW), PW)
        return [
            pltpu.make_async_copy(h.at[0, :, cols], b.at[p], io_sem.at[i, p])
            for i, (h, b) in enumerate(((k_hbm, kb), (v_hbm, vb), (q_hbm, qb), (g_hbm, gb)))
        ]

    def stores(p):
        cols = pl.ds(pl.multiple_of(p * PW, PW), PW)
        return [
            pltpu.make_async_copy(b.at[p], h.at[0, :, cols], io_sem.at[i, p])
            for i, (h, b) in enumerate(((gk_hbm, kb), (gv_hbm, vb), (gq_hbm, qb), (o_hbm, gb)))
        ]

    def hop(kind, src, dst, p, to):
        return pltpu.make_async_remote_copy(
            src_ref=src, dst_ref=dst, send_sem=send_sem.at[kind], recv_sem=recv_sem.at[kind, p],
            device_id=to, device_id_type=MESH,
        )

    def load_kv(p, _):
        for copy in loads(p)[:2]:
            copy.start()
        return 0

    def load_qg(p, _):
        for copy in loads(p)[2:]:
            copy.start()
        return 0

    lax.fori_loop(0, pairs, load_kv, 0)
    lax.fori_loop(0, pairs, load_qg, 0)

    barrier = pltpu.get_barrier_semaphore()
    greet = [sib, ypeer] + steps[:n_dp] + steps[n_dp + 3:]
    for other in greet:
        pl.semaphore_signal(barrier, inc=1, device_id=other, device_id_type=MESH)

    @pl.when(z < nz - 1)
    def _():
        pl.semaphore_signal(barrier, inc=1, device_id=up, device_id_type=MESH)

    @pl.when(z > 0)
    def _():
        pl.semaphore_signal(barrier, inc=1, device_id=down, device_id_type=MESH)

    expected = len(greet) + lax.min(z, 1) + lax.min(nz - 1 - z, 1)
    pl.semaphore_wait(barrier, expected)

    @pl.when(z == 0)
    def _():
        e_in[...] = jnp.zeros_like(e_in)

    @pl.when(z == nz - 1)
    def _():
        te_in[...] = jnp.zeros_like(te_in)

    def to_chip(p, kind, all_ref, in_ref):
        return hop(kind, all_ref.at[1 - c, p], in_ref.at[p], p, sib)

    def chip_total(p, kind, all_ref, in_ref, out_ref, y_ref):
        to_chip(p, kind, all_ref, in_ref).wait_recv()
        out_ref[p] = all_ref[c, p] + in_ref[p]
        hop(kind + 1, out_ref.at[p], y_ref.at[p], p, ypeer).start()

    def along(p, kind, all_ref, in_ref, out_ref, y_ref, e_ref, eo_ref, po_ref, pa_ref, reverse):
        first = nz - 1 if reverse else 0
        last = nz - 1 - first
        to = down if reverse else up
        hop(kind + 1, out_ref.at[p], y_ref.at[p], p, ypeer).wait_recv()

        @pl.when(z != first)
        def _():
            hop(kind + 2, eo_ref.at[p], e_ref.at[p], p, to).wait_recv()

        entering = e_ref[p]
        across = y_ref[p]

        @pl.when(z != last)
        def _():
            eo_ref[p] = entering + (out_ref[p] + across)
            hop(kind + 2, eo_ref.at[p], e_ref.at[p], p, to).start()

        has_y = (y == 0) if reverse else (y == 1)
        mine_later = (c == 0) if reverse else (c == 1)
        base = entering + jnp.where(has_y, across, 0.0)
        po_ref[p] = base + jnp.where(mine_later, 0.0, all_ref[c, p])
        hop(kind + 3, po_ref.at[p], pa_ref.at[c, p], p, sib).start()
        pa_ref[c, p] = base + jnp.where(mine_later, in_ref[p], 0.0)

    fwd = (0, s_all, x_in, c_out, y_in)
    bwd = (4, t_all, tx_in, tc_out, ty_in)

    def prologue(t, _):
        @pl.when(t < pairs)
        def _():
            for copy in loads(t)[:2]:
                copy.wait()
            for j in range(2):
                at = slice(j * HD, (j + 1) * HD)
                s_all[j, t] = tn(kb[t, :, at], vb[t, :, at])
            to_chip(t, 0, s_all, x_in).start()

        @pl.when(t >= LAG_PRO)
        def _():
            chip_total(t - LAG_PRO, *fwd)
        return 0

    lax.fori_loop(0, pairs + LAG_PRO, prologue, 0)

    def forward(p):
        for copy in loads(p)[2:]:
            copy.wait()
        hop(3, p_out.at[p], p_all.at[1 - c, p], p, sib).wait_recv()
        row = lax.broadcasted_iota(jnp.int32, (length, length), 0)
        col = lax.broadcasted_iota(jnp.int32, (length, length), 1)
        causal = row >= col
        two = range(2)
        at = [slice(j * HD, (j + 1) * HD) for j in two]
        lanes = [pl.ds(pl.multiple_of(p * PW + j * HD, HD), HD) for j in two]
        query = [qb[p, :, at[j]] for j in two]
        key_rows = [kb[p, :, at[j]] for j in two]
        value = [vb[p, :, at[j]] for j in two]
        grad = [gb[p, :, at[j]].astype(F32) for j in two]
        prefix = [p_all[j, p].astype(BF16) for j in two]
        gain = [gain_ref[:, lanes[j]] for j in two]
        scores = [jnp.where(causal, nt(query[j], key_rows[j]), 0.0).astype(BF16) for j in two]
        attended = [
            nn(
                jnp.concatenate([scores[j], query[j]], axis=1),
                jnp.concatenate([value[j], prefix[j]], axis=0),
            )
            for j in two
        ]
        inverse = [
            lax.rsqrt(jnp.mean(attended[j] * attended[j], axis=-1, keepdims=True) + EPS) for j in two
        ]
        normed = [attended[j] * inverse[j] for j in two]
        product = [grad[j] * normed[j] for j in two]
        mean = [jnp.mean(product[j] * gain[j], axis=-1, keepdims=True) for j in two]
        dattn = [
            (inverse[j] * (grad[j] * gain[j] - normed[j] * mean[j])).astype(BF16) for j in two
        ]
        gstate = [tn(query[j], dattn[j]) for j in two]
        for j in two:
            t_all[j, p] = gstate[j]
        to_chip(p, 4, t_all, tx_in).start()
        for j in two:
            kept[p, :, at[j]] = dattn[j]
            held[j, p] = scores[j]
            gsum[0, :, lanes[j]] = jnp.sum(product[j], axis=0, keepdims=True)
            gb[p, :, at[j]] = (normed[j] * gain[j]).astype(BF16)
        stores(p)[3].start()

    def final(p):
        hop(7, tp_out.at[p], tp_all.at[1 - c, p], p, sib).wait_recv()
        row = lax.broadcasted_iota(jnp.int32, (length, length), 0)
        col = lax.broadcasted_iota(jnp.int32, (length, length), 1)
        causal = row >= col
        two = range(2)
        at = [slice(j * HD, (j + 1) * HD) for j in two]
        query = [qb[p, :, at[j]] for j in two]
        key_rows = [kb[p, :, at[j]] for j in two]
        value = [vb[p, :, at[j]] for j in two]
        dattn = [kept[p, :, at[j]] for j in two]
        prefix = [p_all[j, p].astype(BF16) for j in two]
        suffix = [tp_all[j, p].astype(BF16) for j in two]
        dscore = [jnp.where(causal, nt(dattn[j], value[j]), 0.0).astype(BF16) for j in two]
        grad_v = [
            (tn(held[j, p], dattn[j]) + nn(key_rows[j], suffix[j])).astype(BF16) for j in two
        ]
        grad_q = [
            nn(
                jnp.concatenate([dscore[j], dattn[j]], axis=1),
                jnp.concatenate([key_rows[j], prefix[j].T], axis=0),
            ).astype(BF16)
            for j in two
        ]
        grad_k = [
            (tn(dscore[j], query[j]) + nt(value[j], suffix[j])).astype(BF16) for j in two
        ]
        for j in two:
            qb[p, :, at[j]] = grad_q[j]
            kb[p, :, at[j]] = grad_k[j]
            vb[p, :, at[j]] = grad_v[j]
        for copy in stores(p)[:3]:
            copy.start()

    def gain_hop(i):
        return pltpu.make_async_remote_copy(
            src_ref=gsum.at[i], dst_ref=grecv.at[i], send_sem=gs_sem.at[i], recv_sem=gr_sem.at[i],
            device_id=steps[i], device_id_type=MESH,
        )

    lag_gz = LAG_GZ + LAG_STEP * (nz - 1 - z)
    after = pairs + LAG_FWD
    lag_fin = lax.max(lag_gz + LAG_FIN, after + LAG_TURN * (z // (nz - 1)))
    gain_at = after
    total = max(
        pairs + max(LAG_GZ + LAG_STEP * (nz - 1) + LAG_FIN, after + LAG_TURN),
        gain_at + 2 * len(steps) + 1,
    )

    def guarded(p, stage):
        @pl.when(jnp.logical_and(p >= 0, p < pairs))
        def _():
            stage(p)

    def main(t, _):
        guarded(t, lambda p: along(p, *fwd, e_in, e_out, p_out, p_all, False))
        guarded(t - LAG_FWD, forward)
        guarded(t - LAG_GY, lambda p: chip_total(p, *bwd))
        guarded(t - lag_gz, lambda p: along(p, *bwd, te_in, te_out, tp_out, tp_all, True))
        guarded(t - lag_fin, final)
        for i in range(len(steps) + 1):
            @pl.when(t == gain_at + 2 * i)
            def _():
                if i > 0:
                    gain_hop(i - 1).wait_recv()
                    gsum[i] = gsum[i - 1] + grecv[i - 1]
                if i < len(steps):
                    gain_hop(i).start()
        return 0

    lax.fori_loop(0, total, main, 0)
    gg_ref[...] = gsum[len(steps)]

    for i in range(len(steps)):
        gain_hop(i).wait_send()
    for kind, all_ref, in_ref, out_ref, y_ref, eo_ref, e_ref, po_ref, pa_ref in (
        (*fwd, e_out, e_in, p_out, p_all),
        (*bwd, te_out, te_in, tp_out, tp_all),
    ):
        hop(kind, all_ref.at[1 - c], in_ref, 0, sib).wait_send()
        hop(kind + 1, out_ref, y_ref, 0, ypeer).wait_send()
        reverse = kind == 4

        @pl.when(z != (0 if reverse else nz - 1))
        def _():
            hop(kind + 2, eo_ref, e_ref, 0, down if reverse else up).wait_send()

        hop(kind + 3, po_ref, pa_ref.at[c], 0, sib).wait_send()

    def finish(p, _):
        for copy in stores(p):
            copy.wait()
        return 0

    lax.fori_loop(0, pairs, finish, 0)


def settle(chunks, *refs):
    sources, total, targets, result, stage, sems = refs[:4], refs[4], refs[5:9], refs[9], refs[10], refs[11]
    rows = stage.shape[1]

    def pair(i):
        a, r = i // chunks, pl.ds((i % chunks) * rows, rows)
        return (
            pltpu.make_async_copy(sources[a].at[0, r], stage.at[i], sems.at[i]),
            pltpu.make_async_copy(stage.at[i], targets[a].at[0, r], sems.at[i]),
        )

    for i in range(4 * chunks):
        pair(i)[0].start()
    result[...] = total[...]
    for i in range(4 * chunks):
        inward, outward = pair(i)
        inward.wait()
        outward.start()
    for i in range(4 * chunks):
        pair(i)[1].wait()


def body(ndp, nctx, queries, keys, values, out_grad, gain):
    _, length, width = queries.shape
    pairs = width // PW
    nsteps = (ndp - 1).bit_length() + (nctx - 1).bit_length()
    tile = pltpu.VMEM((pairs, length, PW), BF16)
    square = pltpu.VMEM((2, pairs, length, length), BF16)
    one = pltpu.VMEM((pairs, HD, HD), F32)
    two = pltpu.VMEM((2, pairs, HD, HD), F32)
    states = [two, one, one, one, one, one, one, two]
    hbm = pl.BlockSpec(memory_space=pl.ANY)
    vmem = pl.BlockSpec(memory_space=pltpu.VMEM)
    big = jax.ShapeDtypeStruct(queries.shape, BF16)
    out = pl.pallas_call(
        functools.partial(kernel, ndp, nctx, pairs),
        out_shape=(big, big, big, big, jax.ShapeDtypeStruct((1, width), F32)),
        in_specs=[hbm, hbm, hbm, hbm, vmem],
        out_specs=(hbm, hbm, hbm, hbm, vmem),
        scratch_shapes=[
            tile, tile, tile, tile, tile, square, *states, *states,
            pltpu.VMEM((nsteps + 1, 1, width), F32),
            pltpu.VMEM((nsteps, 1, width), F32),
            pltpu.SemaphoreType.DMA((4, pairs)),
            pltpu.SemaphoreType.DMA((8,)),
            pltpu.SemaphoreType.DMA((8, pairs)),
            pltpu.SemaphoreType.DMA((nsteps,)),
            pltpu.SemaphoreType.DMA((nsteps,)),
        ],
        compiler_params=pltpu.CompilerParams(
            collective_id=0, has_side_effects=True, vmem_limit_bytes=56 << 20
        ),
        name="lightning",
    )(queries, keys, values, out_grad, gain.reshape(1, width))
    chunks = 4
    out = pl.pallas_call(
        functools.partial(settle, chunks),
        out_shape=(big, big, big, big, jax.ShapeDtypeStruct((1, width), F32)),
        in_specs=[hbm, hbm, hbm, hbm, vmem],
        out_specs=(hbm, hbm, hbm, hbm, vmem),
        scratch_shapes=[
            pltpu.VMEM((4 * chunks, length // chunks, width), BF16),
            pltpu.SemaphoreType.DMA((4 * chunks,)),
        ],
        compiler_params=pltpu.CompilerParams(vmem_limit_bytes=56 << 20),
        name="settle",
    )(*out)
    return (*out[:4], out[4].reshape(width))


def solution(mesh):
    split = P("dp", "ctx", None)
    return jax.shard_map(
        functools.partial(body, mesh.shape["dp"], mesh.shape["ctx"]),
        mesh=mesh,
        in_specs=(split, split, split, split, P()),
        out_specs=(split, split, split, split, P()),
        check_vma=False,
    )
```
